256 devices in a mesh: row: 16 (over y, x), col: 16 (over z, core).
Axes of the slice: x: 4, y: 4, z: 8, core: 2. Of those that a mesh axis runs over, the one named last changes fastest.
Arguments:
- excitation: float32 [16, 16, 2, 32, 1024], P('row', 'col'), may hold values from -6 to 6
- shift_real: float32 [16, 16, 1024], P('row', 'col'), may hold values from 6 to 10
- shift_imag: float32 [16, 16, 1024], P('row', 'col'), may hold values from 1.5 to 4
- local_tiles: bfloat16 [16, 16, 8, 4, 128, 128], P('row', 'col'), may hold values from -0.25 to 0.25
- tile_columns: int32 [16, 16, 8, 4], P('row', 'col'), may hold values from 0 to 7
- coupling: bfloat16 [16, 16, 4, 128, 128], P('row', 'col'), may hold values from -0.5 to 0.5
- send_edges: int32 [16, 16, 4, 128], P('row', 'col'), may hold values from 0 to 1023
- receive_edges: int32 [16, 16, 4, 128], P('row', 'col'), may hold values from 0 to 1023
- local_modes: bfloat16 [16, 16, 96, 1024], P('row', 'col'), may hold values from -0.1875 to 0.1875
- coarse_inverse: bfloat16 [24576, 24576], P('row', 'col'), may hold values from -0.0546875 to 0.0546875
Outputs:
- solution: float32 [16, 16, 2, 32, 1024], P('row', 'col')
- residual: float32 [16, 16, 2, 32, 1024], P('row', 'col')
The draws below stay inside these ranges and needn't reach their ends.
Inputs may be any that keep to these rules, and one draw needn't show every extreme that they name: `tile_columns`: tile column numbers of one subdomain's operator. `send_edges`: edge numbers within the sending subdomain; an edge may repeat. `receive_edges`: edge numbers within the receiving subdomain; an edge may repeat.
All inputs are finite; a program needn't handle non-finite values.
Results may differ from the reference program's by a relative error of at most 0.0003.
Values sent between devices are 32-bit elements; how exact they have to be, the bound alone decides.
No kernel may reach another device: no remote copies, remote signals or barrier semaphores. Data moves between devices by JAX's collectives and lax.ppermute only.
A program may use at most 64 MiB of HBM per device.

```python
import jax
import jax.numpy as jnp
from jax import lax

NE = 1024
TILE = 128
BLOCKS = 4
HALO = 128
MODES = 96
SOURCES = 32
OUTER = 2
PASSES = 2
TILE_ROWS = 8
COARSE = 24576
N_ROW = 16
N_COL = 16


def plant(array, own_key, least, high):
    index_at = [jax.random.randint(jax.random.fold_in(own_key, axis), (), 0, length) for axis, length in enumerate(array.shape)]
    widest = array.shape.index(max(array.shape))
    neighbour = index_at[:widest] + [(index_at[widest] + 1) % array.shape[widest]] + index_at[widest + 1:]
    return array.at[tuple(index_at)].set(least).at[tuple(neighbour)].set(high)


def strengthened(values, rng, source, target, parts, factor):
    def block_of(dim):
        return (jnp.arange(values.shape[dim]) // (values.shape[dim] // parts)).reshape((-1,) + (1,) * (values.ndim - 1 - dim))

    near = jax.random.permutation(rng, parts)[block_of(target)]
    far = (block_of(target) + parts // 2) % parts
    return jnp.where((block_of(source) == near) | (block_of(source) == far), factor * values, values)


def block_levels(rng, extent, split, smallest, largest):
    loudness = 1.0
    for dim, parts in split:
        heights = jax.random.uniform(jax.random.fold_in(jax.random.fold_in(rng, 6), dim), (parts,), jnp.float32, smallest / len(split), largest / len(split))
        loudness = loudness * jnp.repeat(jnp.exp(heights), extent[dim] // parts).reshape((-1,) + (1,) * (len(extent) - 1 - dim))
    return loudness


def bell_draw(stream_key, extent, scale, limit, shards=(), kind=jnp.bfloat16):
    drawn = scale * jax.random.normal(stream_key, extent, jnp.float32)
    if shards:
        drawn = drawn * block_levels(stream_key, extent, shards, -0.22, 0.18)
    return jnp.clip(drawn, -limit, limit).astype(kind)


def heavy_noise(key, dims, spread, reach, split, heavy, kind=jnp.bfloat16):
    values = spread * jax.random.normal(key, dims, jnp.float32)
    if split:
        values = values * block_levels(key, dims, split, -0.22, 0.18)
    return jnp.clip(strengthened(values, jax.random.fold_in(key, 3), *heavy), -reach, reach).astype(kind)


def setup_inputs(seed: int = 0) -> dict:
    streams_of = jax.random.split(jax.random.key(seed), 11)
    excitation = bell_draw(streams_of[0], (N_ROW, N_COL, 2, SOURCES, NE), 1.0, 6.0, ((0, 16), (1, 16)), jnp.float32)
    shift_real = jnp.clip(6.0 + 4.0 * jax.random.uniform(streams_of[1], (N_ROW, N_COL, NE), jnp.float32) ** block_levels(streams_of[1], (N_ROW, N_COL, NE), ((0, 16), (1, 16)), -0.2, 0.2), 6.0, 10.0)
    shift_imag = jnp.clip(1.5 + 2.5 * jax.random.uniform(streams_of[2], (N_ROW, N_COL, NE), jnp.float32) ** block_levels(streams_of[2], (N_ROW, N_COL, NE), ((0, 16), (1, 16)), -0.2, 0.2), 1.5, 4.0)
    local_tiles = bell_draw(streams_of[3], (N_ROW, N_COL, TILE_ROWS, BLOCKS, TILE, TILE), (BLOCKS * TILE) ** -0.5, 0.25, ((0, 16), (1, 16)))
    tile_columns = plant(jax.random.randint(streams_of[4], (N_ROW, N_COL, TILE_ROWS, BLOCKS), 0, NE // TILE), jax.random.fold_in(streams_of[4], 1), 0, (NE // TILE) - 1).astype(jnp.int32)
    coupling = bell_draw(streams_of[5], (N_ROW, N_COL, 4, HALO, HALO), HALO ** -0.5, 0.5, ((0, 16), (1, 16)))
    send_edges = plant(jax.random.randint(streams_of[6], (N_ROW, N_COL, 4, HALO), 0, NE), jax.random.fold_in(streams_of[6], 1), 0, NE - 1).astype(jnp.int32)
    receive_edges = plant(jax.random.randint(streams_of[7], (N_ROW, N_COL, 4, HALO), 0, NE), jax.random.fold_in(streams_of[7], 1), 0, NE - 1).astype(jnp.int32)
    local_modes = bell_draw(streams_of[8], (N_ROW, N_COL, MODES, NE), NE ** -0.5, 0.1875, ((0, 16), (1, 16)))
    coarse_inverse = heavy_noise(streams_of[9], (COARSE, COARSE), COARSE ** -0.5, 0.0546875, ((0, 16), (1, 16)), (1, 0, 16, 2.0))
    return {"excitation": excitation, "shift_real": shift_real, "shift_imag": shift_imag, "local_tiles": local_tiles, "tile_columns": tile_columns, "coupling": coupling, "send_edges": send_edges, "receive_edges": receive_edges, "local_modes": local_modes, "coarse_inverse": coarse_inverse}


def tile_product(arguments):
    block_tiles, block_columns, vector = arguments
    tile_size = block_tiles.shape[-1]
    row_total = vector.shape[0]
    stacked = vector.reshape(row_total, -1, tile_size)
    picked = stacked[:, block_columns, :]
    result = jnp.einsum("stkb,tkab->sta", picked, block_tiles.astype(picked.dtype), precision=lax.Precision.HIGHEST)
    return result.reshape(row_total, -1)


def shift_grid(packed, axis_number, forward):
    length = packed.shape[axis_number]
    shape_list = list(packed.shape)
    shape_list[axis_number] = 1
    zero_block = jnp.zeros(tuple(shape_list), packed.dtype)
    if forward:
        return jnp.concatenate([zero_block, lax.slice_in_dim(packed, 0, length - 1, axis=axis_number)], axis=axis_number)
    return jnp.concatenate([lax.slice_in_dim(packed, 1, length, axis=axis_number), zero_block], axis=axis_number)


def pick_edges(vector, indices):
    return vector[:, :, indices]


def add_edges(vector, indices, values):
    return vector.at[:, :, indices].add(values)


def operate(field, shift_real, shift_imag, local_tiles, tile_columns, coupling, send_edges, receive_edges):
    grid_rows, grid_cols, halves, count_sources, edge_count = field.shape
    flat_field = field.reshape(grid_rows * grid_cols, halves * count_sources, edge_count)
    flat_tiles = local_tiles.reshape((grid_rows * grid_cols,) + local_tiles.shape[2:])
    flat_columns = tile_columns.reshape((grid_rows * grid_cols,) + tile_columns.shape[2:])
    result = lax.map(tile_product, (flat_tiles, flat_columns, flat_field)).reshape(field.shape)
    outgoing = jax.vmap(jax.vmap(pick_edges))(field, send_edges)
    incoming = [
        shift_grid(outgoing[:, :, :, :, 1, :], 0, True),
        shift_grid(outgoing[:, :, :, :, 0, :], 0, False),
        shift_grid(outgoing[:, :, :, :, 3, :], 1, True),
        shift_grid(outgoing[:, :, :, :, 2, :], 1, False),
    ]
    for direction in range(4):
        contribution = jnp.einsum("ijab,ijpsb->ijpsa", coupling[:, :, direction].astype(field.dtype), incoming[direction], precision=lax.Precision.HIGHEST)
        result = jax.vmap(jax.vmap(add_edges))(result, receive_edges[:, :, direction], contribution)
    real_shift = shift_real[:, :, None, :]
    imag_shift = shift_imag[:, :, None, :]
    real_part = real_shift * field[:, :, 0] - imag_shift * field[:, :, 1]
    imag_part = real_shift * field[:, :, 1] + imag_shift * field[:, :, 0]
    return result + jnp.stack([real_part, imag_part], axis=2)


def relaxed(vector, shift_real, shift_imag):
    real_shift = shift_real[:, :, None, :]
    imag_shift = shift_imag[:, :, None, :]
    modulus = real_shift * real_shift + imag_shift * imag_shift
    real_part = (real_shift * vector[:, :, 0] + imag_shift * vector[:, :, 1]) / modulus
    imag_part = (real_shift * vector[:, :, 1] - imag_shift * vector[:, :, 0]) / modulus
    return jnp.stack([real_part, imag_part], axis=2)


def coarse(residual, local_modes, coarse_inverse):
    grid_rows, grid_cols, halves, count_sources, edge_count = residual.shape
    modes_wide = local_modes.astype(residual.dtype)
    projected = jnp.einsum("ijmn,ijpsn->ijmps", modes_wide, residual, precision=lax.Precision.HIGHEST)
    ordered = jnp.transpose(projected, (1, 0, 2, 3, 4)).reshape(-1, halves * count_sources)
    row_blocks = coarse_inverse.reshape(grid_rows, -1, coarse_inverse.shape[1])

    def block_product(block):
        return jnp.dot(block.astype(ordered.dtype), ordered, precision=lax.Precision.HIGHEST)

    coarse_field = lax.map(block_product, row_blocks).reshape(grid_rows, grid_cols, -1, halves, count_sources)
    return jnp.einsum("ijmn,ijmps->ijpsn", modes_wide, coarse_field, precision=lax.Precision.HIGHEST)


def reference(excitation, shift_real, shift_imag, local_tiles, tile_columns, coupling, send_edges, receive_edges, local_modes, coarse_inverse):
    solution = jnp.zeros_like(excitation)
    residual = excitation
    for repeat in range(OUTER):
        update = coarse(residual, local_modes, coarse_inverse)
        for sweep_index in range(PASSES):
            image = operate(update, shift_real, shift_imag, local_tiles, tile_columns, coupling, send_edges, receive_edges)
            update = update + relaxed(residual - image, shift_real, shift_imag)
        solution = solution + update
        residual = excitation - operate(solution, shift_real, shift_imag, local_tiles, tile_columns, coupling, send_edges, receive_edges)
    return solution, residual
```

```python
import jax
import jax.numpy as jnp
from jax import lax
from jax.experimental import pallas as pl
from jax.experimental.pallas import tpu as pltpu
from jax.sharding import PartitionSpec as P

OUTER = 2
N = 16
ROWS = 64
NE = 1024
TILE = 128
MODES = 96
HALF = MODES // 2
F32 = jnp.float32
BF16 = jnp.bfloat16
NT = (((1,), (1,)), ((), ()))
TN = (((0,), (0,)), ((), ()))
NN = (((1,), (0,)), ((), ()))

VMEM = pl.BlockSpec(memory_space=pltpu.VMEM)
SMEM = pl.BlockSpec(memory_space=pltpu.SMEM)


def dot(a, b, dims):
    return lax.dot_general(a, b, dims, preferred_element_type=F32)


def split(x):
    high = x.astype(BF16).astype(F32)
    return high, x - high


def stacked(x):
    high, low = split(x)
    return jnp.concatenate([high.astype(BF16), low.astype(BF16)], axis=0)


def fold_rows(x):
    return x[:ROWS] + x[ROWS:]


def unpack_modes(x):
    high, low = split(x)
    left = lax.broadcasted_iota(jnp.int32, x.shape, 1) < ROWS
    first = jnp.where(left, high, pltpu.roll(low, ROWS, 1))
    second = jnp.where(left, pltpu.roll(high, ROWS, 1), low)
    return first.astype(BF16), second.astype(BF16)


def pack_modes(first, second):
    left = lax.broadcasted_iota(jnp.int32, first.shape, 1) < ROWS
    return jnp.where(left, first + pltpu.roll(first, ROWS, 1), second + pltpu.roll(second, ROWS, 1))


def project(residual, modes):
    wide = dot(modes, stacked(residual), NT)
    return pack_modes(wide[:HALF], wide[HALF:])


def relax(field, real_shift, imag_shift):
    modulus = real_shift * real_shift + imag_shift * imag_shift
    a, b = real_shift / modulus, imag_shift / modulus
    re, im = field[: ROWS // 2], field[ROWS // 2 :]
    return jnp.concatenate([a * re + b * im, a * im - b * re], axis=0)


def spread(packed, out):
    for k in range(N):
        out[k] = packed


def project_kernel(residual, modes, out):
    spread(project(residual[...], modes[...]), out)


def rim_kernel(order, send, modes, pick, rim_modes):
    edge = lax.broadcasted_iota(jnp.int32, (NE, TILE), 0)
    for slot in range(4):
        lanes = slice(slot * TILE, (slot + 1) * TILE)
        chosen = send[pl.ds(order[slot], 1), :]
        pick[:, lanes] = jnp.where(edge == chosen, 1.0, 0.0).astype(BF16)
    rim_modes[...] = dot(modes[...], pick[...], NN).astype(BF16)


def link_kernel(order, receive, coupling, link_high, link_low):
    edge = lax.broadcasted_iota(jnp.int32, (NE, TILE), 0)
    for slot in range(4):
        lanes = slice(slot * TILE, (slot + 1) * TILE)
        target = receive[pl.ds(order[slot], 1), :]
        place = jnp.where(edge == target, 1.0, 0.0).astype(BF16)
        link = dot(place, coupling[order[slot]], NN)
        high, low = split(link)
        link_high[:, lanes] = high.astype(BF16)
        link_low[:, lanes] = low.astype(BF16)


def coarse_kernel(gathered, inverse, out, column):
    for k in range(N):
        first, second = unpack_modes(gathered[k])
        column[k * MODES : k * MODES + HALF, :] = first
        column[k * MODES + HALF : (k + 1) * MODES, :] = second
    step = 4
    for k in range(0, N, step):
        wide = dot(inverse[k * MODES : (k + step) * MODES, :], column[...], NN)
        for m in range(step):
            out[k + m] = pack_modes(wide[m * MODES : m * MODES + HALF], wide[m * MODES + HALF : (m + 1) * MODES])


def start_kernel(parts, rim_modes, field, *rims):
    total = parts[0]
    for k in range(1, N):
        total = total + parts[k]
    first, second = unpack_modes(total)
    both = jnp.concatenate([first, second], axis=0)
    field[...] = both
    rim = fold_rows(dot(both, rim_modes[...], TN))
    for slot in range(4):
        rims[slot][...] = rim[:, slot * TILE : (slot + 1) * TILE]


def tile_product(columns, terms, tiles, scratch, out):
    for k in range(NE // TILE):
        scratch[k] = terms[:, k * TILE : (k + 1) * TILE]
    for t in range(NE // TILE):
        total = None
        for k in range(4):
            part = dot(scratch[columns[t, k]], tiles[t, k], NT)
            total = part if total is None else total + part
        out[:, t * TILE : (t + 1) * TILE] = fold_rows(total)


def first_tiles_kernel(columns, field, modes, tiles, out, scratch):
    update = fold_rows(dot(field[...], modes[...], TN))
    tile_product(columns, stacked(update), tiles, scratch, out)


def tiles_kernel(columns, update, tiles, out, scratch):
    tile_product(columns, stacked(update[...]), tiles, scratch, out)


def applied(inside, local, links, link_high, link_low):
    pieces = [jnp.where(inside[slot] > 0, links[slot][...], 0.0) for slot in range(4)]
    terms = stacked(jnp.concatenate(pieces, axis=1))
    image = local[...] + fold_rows(dot(terms, link_high[...], NT))
    return image + dot(terms[:ROWS], link_low[...], NT)


def sweep_kernel(inside, local, l0, l1, l2, l3, link_high, link_low, pick, residual, real_shift, imag_shift, image, update, *rims):
    value = applied(inside, local, (l0, l1, l2, l3), link_high, link_low)
    image[...] = value
    fresh = relax(residual[...] - value, real_shift[...], imag_shift[...])
    update[...] = fresh
    rim = fold_rows(dot(stacked(fresh), pick[...], NN))
    for slot in range(4):
        rims[slot][...] = rim[:, slot * TILE : (slot + 1) * TILE]


def close_kernel(inside, local, l0, l1, l2, l3, link_high, link_low, image, modes, residual, out):
    value = image[...] - applied(inside, local, (l0, l1, l2, l3), link_high, link_low)
    residual[...] = value
    spread(project(value, modes[...]), out)


def last_kernel(inside, local, l0, l1, l2, l3, link_high, link_low, image, update, before, residual, solution):
    residual[...] = image[...] - applied(inside, local, (l0, l1, l2, l3), link_high, link_low)
    solution[...] = before[...] + update[...]


def shape(dims, dtype=F32):
    return jax.ShapeDtypeStruct(dims, dtype)


def call(kernel, out_shape, in_specs, args, scratch=(), flops=0, name=None):
    outs = out_shape if isinstance(out_shape, (tuple, list)) else (out_shape,)
    moved = sum(a.size * a.dtype.itemsize for a in args) + sum(o.size * jnp.dtype(o.dtype).itemsize for o in outs)
    out_specs = [VMEM] * len(outs)
    return pl.pallas_call(
        kernel,
        out_shape=list(outs),
        in_specs=in_specs,
        out_specs=out_specs,
        scratch_shapes=list(scratch),
        compiler_params=pltpu.CompilerParams(vmem_limit_bytes=16 * 2**20),
        cost_estimate=pl.CostEstimate(flops=flops, bytes_accessed=moved, transcendentals=0),
        name=name,
    )(*args)


EVEN = [(k, k ^ 1) for k in range(N)]
ODD = [(k, (k + 1) % N) for k in range(1, N, 2)] + [((k + 1) % N, k) for k in range(1, N, 2)]


def on_device(
    excitation,
    shift_real,
    shift_imag,
    local_tiles,
    tile_columns,
    coupling,
    send_edges,
    receive_edges,
    local_modes,
    coarse_inverse,
):
    source = excitation.reshape(ROWS, NE)
    real_shift = shift_real.reshape(1, NE)
    imag_shift = shift_imag.reshape(1, NE)
    tiles = local_tiles[0, 0]
    columns = tile_columns[0, 0]
    links = coupling[0, 0]
    send = send_edges[0, 0]
    receive = receive_edges[0, 0]
    modes = local_modes[0, 0]

    row, col = lax.axis_index("row"), lax.axis_index("col")
    row_odd, col_odd = row % 2, col % 2
    order = jnp.stack([1 - row_odd, row_odd, 3 - col_odd, 2 + col_odd]).astype(jnp.int32)
    one = jnp.ones((), jnp.int32)
    row_in = jnp.where((row > 0) & (row < N - 1), 1, 0).astype(jnp.int32)
    col_in = jnp.where((col > 0) & (col < N - 1), 1, 0).astype(jnp.int32)
    inside = jnp.stack([one, row_in, one, col_in])

    rim_shapes = [shape((ROWS, TILE))] * 4
    field_shape = shape((ROWS, NE))
    spread_shape = shape((N, HALF, TILE))

    def exchange(rims):
        return [
            lax.ppermute(rims[0], "row", EVEN),
            lax.ppermute(rims[1], "row", ODD),
            lax.ppermute(rims[2], "col", EVEN),
            lax.ppermute(rims[3], "col", ODD),
        ]

    tile_scratch = [pltpu.VMEM((NE // TILE, 2 * ROWS, TILE), BF16)]
    tile_flops = 2 * 128 * NE * 512
    link_flops = 2 * 192 * 512 * NE

    (packed,) = call(project_kernel, spread_shape, [VMEM] * 2, [source, modes], name="project")
    pick, rim_modes = call(
        rim_kernel, [shape((NE, 4 * TILE), BF16), shape((MODES, 4 * TILE), BF16)], [SMEM, VMEM, VMEM], [order, send, modes], name="rim"
    )
    link_high, link_low = call(
        link_kernel, [shape((NE, 4 * TILE), BF16)] * 2, [SMEM, VMEM, VMEM], [order, receive, links], name="link"
    )

    residual = source
    solution = None
    for repeat in range(OUTER):
        gathered = lax.all_to_all(packed, "row", 0, 0)
        (partial_sums,) = call(
            coarse_kernel, spread_shape, [VMEM] * 2, [gathered, coarse_inverse],
            scratch=[pltpu.VMEM((N * MODES, TILE), BF16)], flops=2 * 1536 * 1536 * 128, name="coarse",
        )
        parts = lax.all_to_all(partial_sums, "col", 0, 0)
        field, *rims = call(
            start_kernel, [shape((MODES, TILE), BF16)] + rim_shapes, [VMEM] * 2, [parts, rim_modes], name="start"
        )
        arrived = exchange(rims)
        (local,) = call(
            first_tiles_kernel, field_shape, [SMEM] + [VMEM] * 3, [columns, field, modes, tiles],
            scratch=tile_scratch, flops=tile_flops, name="tiles0",
        )
        for sweep in range(2):
            image, update, *rims = call(
                sweep_kernel, [field_shape, field_shape] + rim_shapes, [SMEM] + [VMEM] * 11,
                [inside, local, *arrived, link_high, link_low, pick, residual, real_shift, imag_shift],
                flops=link_flops, name="sweep",
            )
            arrived = exchange(rims)
            (local,) = call(
                tiles_kernel, field_shape, [SMEM] + [VMEM] * 2, [columns, update, tiles],
                scratch=tile_scratch, flops=tile_flops, name="tiles",
            )
        common = [inside, local, *arrived, link_high, link_low, image]
        if repeat + 1 < OUTER:
            solution = update
            residual, packed = call(
                close_kernel, [field_shape, spread_shape], [SMEM] + [VMEM] * 9, common + [modes], flops=link_flops, name="close"
            )
        else:
            residual, solution = call(
                last_kernel, [field_shape, field_shape], [SMEM] + [VMEM] * 10, common + [update, solution], flops=link_flops, name="last"
            )
    whole = (1, 1, 2, ROWS // 2, NE)
    return solution.reshape(whole), residual.reshape(whole)


def solution(mesh):
    in_specs = (
        P("row", "col", None, None, None),
        P("row", "col", None),
        P("row", "col", None),
        P("row", "col", None, None, None, None),
        P("row", "col", None, None),
        P("row", "col", None, None, None),
        P("row", "col", None, None),
        P("row", "col", None, None),
        P("row", "col", None, None),
        P("row", "col"),
    )
    out_specs = (P("row", "col", None, None, None), P("row", "col", None, None, None))
    return jax.shard_map(on_device, mesh=mesh, in_specs=in_specs, out_specs=out_specs, check_vma=False)
```

```python
import jax
import jax.numpy as jnp
from jax import lax
from jax.experimental import pallas as pl
from jax.experimental.pallas import tpu as pltpu
from jax.sharding import PartitionSpec as P

OUTER = 2
N = 16
ROWS = 64
NE = 1024
TILE = 128
MODES = 96
HALF = MODES // 2
F32 = jnp.float32
BF16 = jnp.bfloat16
NT = (((1,), (1,)), ((), ()))
TN = (((0,), (0,)), ((), ()))
NN = (((1,), (0,)), ((), ()))

VMEM = pl.BlockSpec(memory_space=pltpu.VMEM)
SMEM = pl.BlockSpec(memory_space=pltpu.SMEM)
HBM = pl.BlockSpec(memory_space=pltpu.HBM)


def dot(a, b, dims):
    return lax.dot_general(a, b, dims, preferred_element_type=F32)


def split(x):
    high = x.astype(BF16).astype(F32)
    return high, x - high


def stacked(x):
    high, low = split(x)
    return jnp.concatenate([high.astype(BF16), low.astype(BF16)], axis=0)


def fold_rows(x):
    return x[:ROWS] + x[ROWS:]


def unpack_modes(x):
    high, low = split(x)
    left = lax.broadcasted_iota(jnp.int32, x.shape, 1) < ROWS
    first = jnp.where(left, high, pltpu.roll(low, ROWS, 1))
    second = jnp.where(left, pltpu.roll(high, ROWS, 1), low)
    return first.astype(BF16), second.astype(BF16)


def pack_modes(first, second):
    left = lax.broadcasted_iota(jnp.int32, first.shape, 1) < ROWS
    return jnp.where(left, first + pltpu.roll(first, ROWS, 1), second + pltpu.roll(second, ROWS, 1))


def project(residual, modes):
    wide = dot(modes, stacked(residual), NT)
    return pack_modes(wide[:HALF], wide[HALF:])


def coefficients(real_shift, imag_shift):
    modulus = real_shift * real_shift + imag_shift * imag_shift
    return real_shift / modulus, imag_shift / modulus


def relax(field, a, b):
    re, im = field[: ROWS // 2], field[ROWS // 2 :]
    return jnp.concatenate([a * re + b * im, a * im - b * re], axis=0)


def spread(packed, out):
    for k in range(N):
        out[k] = packed


def scattered(terms, place):
    return fold_rows(dot(terms, place, NT))


def put_rims(rim, rims):
    for slot in range(4):
        rims[slot][...] = rim[:, slot * TILE : (slot + 1) * TILE]


def project_kernel(residual, modes, out, residual_here, modes_here, sems):
    first = pltpu.make_async_copy(residual, residual_here, sems.at[0])
    second = pltpu.make_async_copy(modes, modes_here, sems.at[1])
    first.start()
    second.start()
    first.wait()
    second.wait()
    spread(project(residual_here[...], modes_here[...]), out)


def one_hot(order, edges, out):
    edge = lax.broadcasted_iota(jnp.int32, (NE, TILE), 0)
    for slot in range(4):
        chosen = edges[pl.ds(order[slot], 1), :]
        out[:, slot * TILE : (slot + 1) * TILE] = jnp.where(edge == chosen, 1.0, 0.0).astype(BF16)


def rim_kernel(order, send, modes, pick, rim_modes):
    one_hot(order, send, pick)
    rim_modes[...] = dot(modes[...], pick[...], NN).astype(BF16)


def link_kernel(order, send, receive, pick, real_shift, imag_shift, cross, coef, rim_coef):
    rows = [receive[pl.ds(order[slot], 1), :] for slot in range(4)]
    targets = jnp.concatenate(rows + rows, axis=0).T
    for slot in range(4):
        chosen = send[pl.ds(order[slot], 1), :]
        for other in range(4):
            same = targets[:, other : other + 1] == chosen
            cross[other * TILE : (other + 1) * TILE, slot * TILE : (slot + 1) * TILE] = jnp.where(same, 1.0, 0.0).astype(BF16)
    a, b = coefficients(real_shift[...], imag_shift[...])
    both = jnp.concatenate([a, b, jnp.zeros((6, NE), F32)], axis=0)
    coef[...] = both
    total = None
    rest = both
    for _ in range(3):
        term = rest.astype(BF16)
        part = dot(term, pick[...], NN)
        total = part if total is None else total + part
        rest = rest - term.astype(F32)
    rim_coef[...] = total


def place_kernel(order, receive, modes, place, place_modes):
    one_hot(order, receive, place)
    place_modes[...] = dot(modes[...], place[...], NN).astype(BF16)


def coarse_product(wide, core, keep, give, z):
    pair = []
    for m in range(2):
        base = m * MODES
        pair.append(pack_modes(wide[base : base + HALF], wide[base + HALF : base + MODES]))
    keep[z] = jnp.where(core == 0, pair[0], pair[1])
    give[z] = jnp.where(core == 0, pair[1], pair[0])


def gather_column(gathered, column):
    for k in range(N):
        first, second = unpack_modes(gathered[k])
        column[k * MODES : k * MODES + HALF, :] = first
        column[k * MODES + HALF : (k + 1) * MODES, :] = second


CHUNK = 4 * MODES


def coarse_chunk(k, inverse, column, core, keep, give):
    wide = dot(inverse[k * CHUNK : (k + 1) * CHUNK, :], column[...], NN)
    for m in range(2):
        coarse_product(wide[2 * m * MODES : (2 * m + 2) * MODES], core, keep, give, 2 * k + m)


def coarse_kernel(core, gathered, inverse, keep, give, column):
    gather_column(gathered, column)
    for k in range(4):
        coarse_chunk(k, inverse, column, core[0], keep, give)


def start_kernel(parts, rim_modes, field, *rims):
    total = parts[0]
    for k in range(1, N // 2):
        total = total + parts[k]
    first, second = unpack_modes(total)
    both = jnp.concatenate([first, second], axis=0)
    field[...] = both
    put_rims(fold_rows(dot(both, rim_modes[...], TN)), rims)


def tile_product(columns, terms, tiles, scratch):
    for k in range(NE // TILE):
        scratch[k] = terms[:, k * TILE : (k + 1) * TILE]
    pieces = []
    for t in range(NE // TILE):
        taken = jnp.concatenate([scratch[columns[t, k]] for k in range(4)], axis=1)
        stored = jnp.concatenate([tiles[t, k] for k in range(4)], axis=1)
        pieces.append(fold_rows(dot(taken, stored, NT)))
    return jnp.concatenate(pieces, axis=1)


def open_tail(columns, field, modes, tiles, pick, residual, local, rim_rest, scratch):
    update = fold_rows(dot(field[...], modes[...], TN))
    image = tile_product(columns, stacked(update), tiles, scratch)
    local[...] = image
    rim_rest[...] = fold_rows(dot(stacked(residual - image), pick[...], NN))


def open_kernel(columns, field, modes, tiles, pick, residual, local, rim_rest, scratch):
    open_tail(columns, field, modes, tiles, pick, residual[...], local, rim_rest, scratch)


def reopen_kernel(columns, field, modes, tiles, pick, rest, terms, place, residual, local, rim_rest, scratch):
    value = rest[...] - scattered(terms[...], place[...])
    residual[...] = value
    open_tail(columns, field, modes, tiles, pick, value, local, rim_rest, scratch)


def middle_kernel(columns, tiles, pick, place, residual, local, terms, coef, after, rim_rest, scratch):
    whole = residual[...] - (local[...] + scattered(terms[...], place[...]))
    update = relax(whole, coef[0:1, :], coef[1:2, :])
    image = tile_product(columns, stacked(update), tiles, scratch)
    after[...] = image
    rim_rest[...] = fold_rows(dot(stacked(residual[...] - image), pick[...], NN))


def finish(columns, tiles, place, residual, local, terms, coef, scratch):
    applied = local[...] + scattered(terms[...], place[...])
    update = relax(residual[...] - applied, coef[0:1, :], coef[1:2, :])
    return update, applied - tile_product(columns, stacked(update), tiles, scratch)


def finish_kernel(columns, tiles, place, residual, local, terms, coef, modes, solution, rest, projected, scratch):
    update, value = finish(columns, tiles, place, residual, local, terms, coef, scratch)
    solution[...] = update
    rest[...] = value
    projected[...] = project(value, modes[...])


def finish_last_kernel(columns, tiles, place, residual, local, terms, coef, before, solution, rest, scratch):
    update, value = finish(columns, tiles, place, residual, local, terms, coef, scratch)
    solution[...] = before[...] + update
    rest[...] = value


def coupled(order, inside, links, coupling):
    pieces = []
    for slot in range(4):
        offered = jnp.where(inside[slot] > 0, links[slot][...], 0.0)
        pieces.append(fold_rows(dot(stacked(offered), coupling[order[slot]], NT)))
    return stacked(jnp.concatenate(pieces, axis=1))


def sweep_kernel(order, inside, l0, l1, l2, l3, coupling, cross, rim_rest, rim_coef, terms, *rims):
    value = coupled(order, inside, (l0, l1, l2, l3), coupling)
    terms[...] = value
    rest = rim_rest[...] - fold_rows(dot(value, cross[...], NN))
    put_rims(relax(rest, rim_coef[0:1, :], rim_coef[1:2, :]), rims)


def close_kernel(order, inside, l0, l1, l2, l3, coupling, place_modes, projected, terms, out):
    value = coupled(order, inside, (l0, l1, l2, l3), coupling)
    terms[...] = value
    wide = dot(place_modes[...], value, NT)
    spread(projected[...] - pack_modes(wide[:HALF], wide[HALF:]), out)


def last_kernel(order, inside, l0, l1, l2, l3, coupling, place, rest, residual, value, sems):
    terms = coupled(order, inside, (l0, l1, l2, l3), coupling)
    copies = []
    for k in range(4):
        lanes = pl.ds(k * 256, 256)
        value[:, lanes] = rest[:, lanes] - scattered(terms, place[k * 256 : (k + 1) * 256, :])
        copies.append(pltpu.make_async_copy(value.at[:, lanes], residual.at[:, lanes], sems.at[k]))
        copies[-1].start()
    for copy in copies:
        copy.wait()


def shape(dims, dtype=F32):
    return jax.ShapeDtypeStruct(dims, dtype)


def held(dims, dtype=F32):
    return pltpu.VMEM(dims, dtype)


def in_hbm(x):
    return pltpu.with_memory_space_constraint(x, pltpu.HBM)


def call(kernel, out_shape, in_specs, args, scratch=(), us=1.0, name=None, limit=16, out_specs=None):
    moved = 2**20
    flops = int(us * 1.1e9)
    return pl.pallas_call(
        kernel,
        out_shape=list(out_shape),
        in_specs=in_specs,
        out_specs=out_specs or [VMEM] * len(out_shape),
        scratch_shapes=list(scratch),
        compiler_params=pltpu.CompilerParams(vmem_limit_bytes=limit * 2**20),
        cost_estimate=pl.CostEstimate(flops=flops, bytes_accessed=moved, transcendentals=0),
        name=name,
    )(*args)


EVEN = [(k, k ^ 1) for k in range(N)]
ODD = [(k, (k + 1) % N) for k in range(1, N, 2)] + [((k + 1) % N, k) for k in range(1, N, 2)]
SAME_CORE = [list(range(core, N, 2)) for core in range(2)]


def on_device(
    excitation,
    shift_real,
    shift_imag,
    local_tiles,
    tile_columns,
    coupling,
    send_edges,
    receive_edges,
    local_modes,
    coarse_inverse,
):
    source = excitation.reshape(ROWS, NE)
    real_shift = shift_real.reshape(1, NE)
    imag_shift = shift_imag.reshape(1, NE)
    tiles = local_tiles[0, 0]
    columns = tile_columns[0, 0]
    links = coupling[0, 0]
    send = send_edges[0, 0]
    receive = receive_edges[0, 0]
    modes = local_modes[0, 0]

    row, col = lax.axis_index("row"), lax.axis_index("col")
    row_odd, col_odd = row % 2, col % 2
    order = jnp.stack([row_odd, 2 + col_odd, 1 - row_odd, 3 - col_odd]).astype(jnp.int32)
    one = jnp.ones((), jnp.int32)
    row_in = jnp.where((row > 0) & (row < N - 1), 1, 0).astype(jnp.int32)
    col_in = jnp.where((col > 0) & (col < N - 1), 1, 0).astype(jnp.int32)
    inside = jnp.stack([row_in, col_in, one, one])
    core = col_odd.astype(jnp.int32).reshape(1)

    rim_shapes = [shape((ROWS, TILE))] * 4
    field_shape = held((ROWS, NE))
    rim_shape = held((ROWS, 4 * TILE))
    terms_shape = held((2 * ROWS, 4 * TILE), BF16)
    hot_shape = held((NE, 4 * TILE), BF16)
    spread_shape = shape((N, HALF, TILE))
    half_shape = shape((N // 2, HALF, TILE))

    def exchange(rims):
        return [
            lax.ppermute(rims[0], "row", ODD),
            lax.ppermute(rims[1], "col", ODD),
            lax.ppermute(rims[2], "row", EVEN),
            lax.ppermute(rims[3], "col", EVEN),
        ]

    tile_scratch = [pltpu.VMEM((NE // TILE, 2 * ROWS, TILE), BF16)]
    column_scratch = pltpu.VMEM((N * MODES, TILE), BF16)

    packed, residual, modes = call(
        project_kernel, [spread_shape, field_shape, held((MODES, NE), BF16)], [HBM] * 2, [in_hbm(source), in_hbm(modes)],
        scratch=[pltpu.SemaphoreType.DMA((2,))], name="project", us=8.0,
    )
    packed, order, inside, core = lax.optimization_barrier((packed, order, inside, core))

    for repeat in range(OUTER):
        gathered = lax.all_to_all(packed, "row", 0, 0)
        keep, give = call(
            coarse_kernel, [half_shape] * 2, [SMEM, VMEM, VMEM], [core, gathered, coarse_inverse],
            scratch=[column_scratch], us=1.6, name="coarse",
        )
        pair_sum = keep + lax.ppermute(give, "col", EVEN)
        if repeat == 0:
            now, _ = lax.optimization_barrier((order, keep))
            pick, rim_modes = call(
                rim_kernel, [hot_shape, held((MODES, 4 * TILE), BF16)], [SMEM, VMEM, VMEM], [now, send, modes], name="rim"
            )
            pair_sum, pick, rim_modes = lax.optimization_barrier((pair_sum, pick, rim_modes))
        parts = lax.all_to_all(pair_sum, "col", 0, 0, axis_index_groups=SAME_CORE)
        field, *rims = call(
            start_kernel, [held((MODES, TILE), BF16)] + rim_shapes, [VMEM] * 2, [parts, rim_modes], name="start"
        )
        arrived = exchange(rims)
        if repeat == 0:
            now, _ = lax.optimization_barrier((order, field))
            columns = jnp.where(now[0] >= 0, columns, 0)
            cross, coef, rim_coef = call(
                link_kernel, [held((4 * TILE, 4 * TILE), BF16), held((8, NE)), held((8, 4 * TILE))],
                [SMEM] + [VMEM] * 5, [now, send, receive, pick, real_shift, imag_shift], name="link", us=0.7,
            )
            local, rim_rest = call(
                open_kernel, [field_shape, rim_shape], [SMEM] + [VMEM] * 5, [columns, field, modes, tiles, pick, residual],
                scratch=tile_scratch, us=1.6, name="open",
            )
        else:
            residual, local, rim_rest = call(
                reopen_kernel, [field_shape, field_shape, rim_shape], [SMEM] + [VMEM] * 7,
                [columns, field, modes, tiles, pick, rest, terms, place],
                scratch=tile_scratch, us=1.6, name="reopen",
            )
        for sweep in range(2):
            terms, *rims = call(
                sweep_kernel, [terms_shape] + rim_shapes, [SMEM, SMEM] + [VMEM] * 8,
                [order, inside, *arrived, links, cross, rim_rest, rim_coef], us=0.9, name="sweep",
            )
            arrived = exchange(rims)
            if repeat == 0 and sweep == 0:
                now, _ = lax.optimization_barrier((order, terms))
                place, place_modes = call(
                    place_kernel, [hot_shape, held((MODES, 4 * TILE), BF16)], [SMEM, VMEM, VMEM], [now, receive, modes], name="place"
                )
            common = [residual, local, terms, coef]
            if sweep == 0:
                local, rim_rest = call(
                    middle_kernel, [field_shape, rim_shape], [SMEM] + [VMEM] * 7, [columns, tiles, pick, place] + common,
                    scratch=tile_scratch, us=1.6, name="middle",
                )
            elif repeat + 1 < OUTER:
                solution, rest, projected = call(
                    finish_kernel, [field_shape, field_shape, held((HALF, TILE))], [SMEM] + [VMEM] * 7,
                    [columns, tiles, place] + common + [modes], scratch=tile_scratch, us=1.6, name="finish",
                )
            else:
                solution, rest = call(
                    finish_last_kernel, [shape((ROWS, NE)), field_shape], [SMEM] + [VMEM] * 7,
                    [columns, tiles, place] + common + [solution], scratch=tile_scratch, us=1.6, name="finish_last",
                )
        if repeat + 1 < OUTER:
            terms, packed = call(
                close_kernel, [terms_shape, spread_shape], [SMEM, SMEM] + [VMEM] * 7,
                [order, inside, *arrived, links, place_modes, projected], us=0.9, name="close",
            )
        else:
            (residual,) = call(
                last_kernel, [shape((ROWS, NE))], [SMEM, SMEM] + [VMEM] * 7, [order, inside, *arrived, links, place, rest],
                us=0.9, name="last", out_specs=[HBM],
                scratch=[pltpu.VMEM((ROWS, NE), F32), pltpu.SemaphoreType.DMA((4,))],
            )
    whole = (1, 1, 2, ROWS // 2, NE)
    return solution.reshape(whole), residual.reshape(whole)


def solution(mesh):
    in_specs = (
        P("row", "col", None, None, None),
        P("row", "col", None),
        P("row", "col", None),
        P("row", "col", None, None, None, None),
        P("row", "col", None, None),
        P("row", "col", None, None, None),
        P("row", "col", None, None),
        P("row", "col", None, None),
        P("row", "col", None, None),
        P("row", "col"),
    )
    out_specs = (P("row", "col", None, None, None), P("row", "col", None, None, None))
    return jax.shard_map(on_device, mesh=mesh, in_specs=in_specs, out_specs=out_specs, check_vma=False)
```

```python
import jax
import jax.numpy as jnp
from jax import lax
from jax.experimental import pallas as pl
from jax.experimental.pallas import tpu as pltpu
from jax.sharding import PartitionSpec as P

OUTER = 2
N = 16
ROWS = 64
NE = 1024
TILE = 128
MODES = 96
HALF = MODES // 2
F32 = jnp.float32
BF16 = jnp.bfloat16
NT = (((1,), (1,)), ((), ()))
TN = (((0,), (0,)), ((), ()))
NN = (((1,), (0,)), ((), ()))

VMEM = pl.BlockSpec(memory_space=pltpu.VMEM)
SMEM = pl.BlockSpec(memory_space=pltpu.SMEM)
HBM = pl.BlockSpec(memory_space=pltpu.HBM)


def dot(a, b, dims):
    return lax.dot_general(a, b, dims, preferred_element_type=F32)


def split(x):
    high = x.astype(BF16).astype(F32)
    return high, x - high


def stacked(x):
    high, low = split(x)
    return jnp.concatenate([high.astype(BF16), low.astype(BF16)], axis=0)


def fold_rows(x):
    return x[:ROWS] + x[ROWS:]


def unpack_modes(x):
    high, low = split(x)
    left = lax.broadcasted_iota(jnp.int32, x.shape, 1) < ROWS
    first = jnp.where(left, high, pltpu.roll(low, ROWS, 1))
    second = jnp.where(left, pltpu.roll(high, ROWS, 1), low)
    return first.astype(BF16), second.astype(BF16)


def pack_modes(first, second):
    left = lax.broadcasted_iota(jnp.int32, first.shape, 1) < ROWS
    return jnp.where(left, first + pltpu.roll(first, ROWS, 1), second + pltpu.roll(second, ROWS, 1))


def project(residual, modes):
    wide = dot(modes, stacked(residual), NT)
    return pack_modes(wide[:HALF], wide[HALF:])


def coefficients(real_shift, imag_shift):
    modulus = real_shift * real_shift + imag_shift * imag_shift
    return real_shift / modulus, imag_shift / modulus


def relax(field, a, b):
    re, im = field[: ROWS // 2], field[ROWS // 2 :]
    return jnp.concatenate([a * re + b * im, a * im - b * re], axis=0)


def spread(packed, out):
    for k in range(N):
        out[k] = packed


def scattered(terms, place):
    return fold_rows(dot(terms, place, NT))


def put_rims(rim, rims):
    for slot in range(4):
        rims[slot][...] = rim[:, slot * TILE : (slot + 1) * TILE]


def project_kernel(residual, modes, out, residual_here, modes_here, sems):
    first = pltpu.make_async_copy(residual, residual_here, sems.at[0])
    second = pltpu.make_async_copy(modes, modes_here, sems.at[1])
    first.start()
    second.start()
    first.wait()
    second.wait()
    spread(project(residual_here[...], modes_here[...]), out)


def one_hot(order, edges, out):
    edge = lax.broadcasted_iota(jnp.int32, (NE, TILE), 0)
    for slot in range(4):
        chosen = edges[pl.ds(order[slot], 1), :]
        out[:, slot * TILE : (slot + 1) * TILE] = jnp.where(edge == chosen, 1.0, 0.0).astype(BF16)


def rim_kernel(order, send, modes, pick, rim_modes):
    one_hot(order, send, pick)
    rim_modes[...] = dot(modes[...], pick[...], NN).astype(BF16)


def link_kernel(order, send, receive, pick, real_shift, imag_shift, coupling, cross, coef, rim_coef, links):
    for slot in range(4):
        links[slot] = coupling[order[slot]].astype(F32).T.astype(BF16)
    rows = [receive[pl.ds(order[slot], 1), :] for slot in range(4)]
    targets = jnp.concatenate(rows + rows, axis=0).T
    for slot in range(4):
        chosen = send[pl.ds(order[slot], 1), :]
        for other in range(4):
            same = targets[:, other : other + 1] == chosen
            cross[other * TILE : (other + 1) * TILE, slot * TILE : (slot + 1) * TILE] = jnp.where(same, 1.0, 0.0).astype(BF16)
    a, b = coefficients(real_shift[...], imag_shift[...])
    both = jnp.concatenate([a, b, jnp.zeros((6, NE), F32)], axis=0)
    coef[...] = both
    total = None
    rest = both
    for _ in range(3):
        term = rest.astype(BF16)
        part = dot(term, pick[...], NN)
        total = part if total is None else total + part
        rest = rest - term.astype(F32)
    rim_coef[...] = total


def place_kernel(order, receive, modes, place, place_modes):
    one_hot(order, receive, place)
    place_modes[...] = dot(modes[...], place[...], NN).astype(BF16)


def gather_column(gathered, column):
    for k in range(N):
        first, second = unpack_modes(gathered[k])
        column[k * MODES : k * MODES + HALF, :] = first
        column[k * MODES + HALF : (k + 1) * MODES, :] = second


def half_product(parity, inverse, column, out):
    for k in range(0, N // 2, 4):
        starts = [pl.multiple_of((2 * z + parity) * MODES, MODES) for z in range(k, k + 4)]
        rows = jnp.concatenate([inverse[pl.ds(start, MODES), :] for start in starts], axis=0)
        wide = dot(rows, column[...], NN)
        for z in range(4):
            base = z * MODES
            out[k + z] = pack_modes(wide[base : base + HALF], wide[base + HALF : base + MODES])


def give_kernel(core, gathered, inverse, give, column):
    gather_column(gathered, column)
    half_product(1 - core[0], inverse, column, give)


def keep_kernel(core, column, inverse, keep):
    half_product(core[0], inverse, column, keep)


def start_kernel(parts, rim_modes, field, *rims):
    total = parts[0]
    for k in range(1, N // 2):
        total = total + parts[k]
    first, second = unpack_modes(total)
    both = jnp.concatenate([first, second], axis=0)
    field[...] = both
    put_rims(fold_rows(dot(both, rim_modes[...], TN)), rims)


def tile_product(columns, terms, tiles, scratch):
    for k in range(NE // TILE):
        scratch[k] = terms[:, k * TILE : (k + 1) * TILE]
    pieces = []
    for t in range(NE // TILE):
        taken = jnp.concatenate([scratch[columns[t, k]] for k in range(4)], axis=1)
        stored = jnp.concatenate([tiles[t, k] for k in range(4)], axis=1)
        pieces.append(fold_rows(dot(taken, stored, NT)))
    return jnp.concatenate(pieces, axis=1)


def open_tail(columns, field, modes, tiles, pick, residual, local, rim_rest, scratch):
    update = fold_rows(dot(field[...], modes[...], TN))
    image = tile_product(columns, stacked(update), tiles, scratch)
    local[...] = image
    rim_rest[...] = fold_rows(dot(stacked(residual - image), pick[...], NN))


def open_kernel(columns, field, modes, tiles, pick, residual, local, rim_rest, scratch):
    open_tail(columns, field, modes, tiles, pick, residual[...], local, rim_rest, scratch)


def reopen_kernel(columns, field, modes, tiles, pick, rest, terms, place, residual, local, rim_rest, scratch):
    value = rest[...] - scattered(terms[...], place[...])
    residual[...] = value
    open_tail(columns, field, modes, tiles, pick, value, local, rim_rest, scratch)


def middle_kernel(columns, tiles, pick, place, residual, local, terms, coef, after, rim_rest, scratch):
    whole = residual[...] - (local[...] + scattered(terms[...], place[...]))
    update = relax(whole, coef[0:1, :], coef[1:2, :])
    image = tile_product(columns, stacked(update), tiles, scratch)
    after[...] = image
    rim_rest[...] = fold_rows(dot(stacked(residual[...] - image), pick[...], NN))


def finish(columns, tiles, place, residual, local, terms, coef, scratch):
    applied = local[...] + scattered(terms[...], place[...])
    update = relax(residual[...] - applied, coef[0:1, :], coef[1:2, :])
    return update, applied - tile_product(columns, stacked(update), tiles, scratch)


def finish_kernel(columns, tiles, place, residual, local, terms, coef, modes, solution, rest, projected, scratch):
    update, value = finish(columns, tiles, place, residual, local, terms, coef, scratch)
    solution[...] = update
    rest[...] = value
    projected[...] = project(value, modes[...])


def finish_last_kernel(columns, tiles, place, residual, local, terms, coef, before, solution, rest, scratch):
    update, value = finish(columns, tiles, place, residual, local, terms, coef, scratch)
    solution[...] = before[...] + update
    rest[...] = value


def coupled(inside, rims, links):
    pieces = []
    for slot in range(4):
        offered = jnp.where(inside[slot] > 0, rims[slot][...], 0.0)
        pieces.append(fold_rows(dot(stacked(offered), links[slot], NN)))
    return stacked(jnp.concatenate(pieces, axis=1))


def sweep_kernel(inside, l0, l1, l2, l3, links, cross, rim_rest, rim_coef, terms, *rims):
    value = coupled(inside, (l0, l1, l2, l3), links)
    terms[...] = value
    rest = rim_rest[...] - fold_rows(dot(value, cross[...], NN))
    put_rims(relax(rest, rim_coef[0:1, :], rim_coef[1:2, :]), rims)


def close_kernel(inside, l0, l1, l2, l3, links, place_modes, projected, terms, out):
    value = coupled(inside, (l0, l1, l2, l3), links)
    terms[...] = value
    wide = dot(place_modes[...], value, NT)
    spread(projected[...] - pack_modes(wide[:HALF], wide[HALF:]), out)


def last_kernel(inside, l0, l1, l2, l3, links, place, rest, residual, value, sems):
    terms = coupled(inside, (l0, l1, l2, l3), links)
    copies = []
    for k in range(4):
        lanes = pl.ds(k * 256, 256)
        value[:, lanes] = rest[:, lanes] - scattered(terms, place[k * 256 : (k + 1) * 256, :])
        copies.append(pltpu.make_async_copy(value.at[:, lanes], residual.at[:, lanes], sems.at[k]))
        copies[-1].start()
    for copy in copies:
        copy.wait()


def shape(dims, dtype=F32):
    return jax.ShapeDtypeStruct(dims, dtype)


def held(dims, dtype=F32):
    return pltpu.VMEM(dims, dtype)


def in_hbm(x):
    return pltpu.with_memory_space_constraint(x, pltpu.HBM)


def call(kernel, out_shape, in_specs, args, scratch=(), us=1.0, name=None, limit=16, out_specs=None):
    moved = 2**20
    flops = int(us * 1.1e9)
    return pl.pallas_call(
        kernel,
        out_shape=list(out_shape),
        in_specs=in_specs,
        out_specs=out_specs or [VMEM] * len(out_shape),
        scratch_shapes=list(scratch),
        compiler_params=pltpu.CompilerParams(vmem_limit_bytes=limit * 2**20),
        cost_estimate=pl.CostEstimate(flops=flops, bytes_accessed=moved, transcendentals=0),
        name=name,
    )(*args)


EVEN = [(k, k ^ 1) for k in range(N)]


def odd(k):
    return k - 1 if k % 2 == 0 else k + 1


def permutation(partner):
    return [(N * i + j, N * partner(i, j)[0] + partner(i, j)[1]) for i in range(N) for j in range(N)]


ROW_ODD = permutation(lambda i, j: (i, j ^ 1) if i in (0, N - 1) else (odd(i), j))
COL_ODD = permutation(lambda i, j: (i ^ 1, j) if j in (0, N - 1) else (i, odd(j)))
SAME_CORE = [list(range(core, N, 2)) for core in range(2)]


def on_device(
    excitation,
    shift_real,
    shift_imag,
    local_tiles,
    tile_columns,
    coupling,
    send_edges,
    receive_edges,
    local_modes,
    coarse_inverse,
):
    source = excitation.reshape(ROWS, NE)
    real_shift = shift_real.reshape(1, NE)
    imag_shift = shift_imag.reshape(1, NE)
    tiles = local_tiles[0, 0]
    columns = tile_columns[0, 0]
    send = send_edges[0, 0]
    receive = receive_edges[0, 0]
    modes = local_modes[0, 0]

    row, col = lax.axis_index("row"), lax.axis_index("col")
    row_odd, col_odd = row % 2, col % 2
    order = jnp.stack([row_odd, 2 + col_odd, 1 - row_odd, 3 - col_odd]).astype(jnp.int32)
    one = jnp.ones((), jnp.int32)
    row_in = jnp.where((row > 0) & (row < N - 1), 1, 0).astype(jnp.int32)
    col_in = jnp.where((col > 0) & (col < N - 1), 1, 0).astype(jnp.int32)
    inside = jnp.stack([row_in, col_in, one, one])
    core = col_odd.astype(jnp.int32).reshape(1)

    rim_shapes = [shape((ROWS, TILE))] * 4
    field_shape = held((ROWS, NE))
    rim_shape = held((ROWS, 4 * TILE))
    terms_shape = held((2 * ROWS, 4 * TILE), BF16)
    hot_shape = held((NE, 4 * TILE), BF16)
    spread_shape = shape((N, HALF, TILE))
    half_shape = shape((N // 2, HALF, TILE))

    def exchange(rims):
        return [
            lax.ppermute(rims[0], ("row", "col"), ROW_ODD),
            lax.ppermute(rims[1], ("row", "col"), COL_ODD),
            lax.ppermute(rims[2], "row", EVEN),
            lax.ppermute(rims[3], "col", EVEN),
        ]

    tile_scratch = [pltpu.VMEM((NE // TILE, 2 * ROWS, TILE), BF16)]

    packed, residual, modes = call(
        project_kernel, [spread_shape, field_shape, held((MODES, NE), BF16)], [HBM] * 2, [in_hbm(source), in_hbm(modes)],
        scratch=[pltpu.SemaphoreType.DMA((2,))], name="project", us=8.0,
    )
    packed, order, inside, core = lax.optimization_barrier((packed, order, inside, core))

    for repeat in range(OUTER):
        gathered = lax.all_to_all(packed, "row", 0, 0)
        give, column = call(
            give_kernel, [half_shape, held((N * MODES, TILE), BF16)], [SMEM, VMEM, VMEM], [core, gathered, coarse_inverse],
            us=0.9, name="give",
        )
        (keep,) = call(
            keep_kernel, [half_shape], [SMEM, VMEM, VMEM], [core, column, coarse_inverse], us=0.9, name="keep",
        )
        pair_sum = keep + lax.ppermute(give, "col", EVEN)
        if repeat == 0:
            now, _ = lax.optimization_barrier((order, give))
            pick, rim_modes = call(
                rim_kernel, [hot_shape, held((MODES, 4 * TILE), BF16)], [SMEM, VMEM, VMEM], [now, send, modes], name="rim"
            )
            pair_sum, pick, rim_modes = lax.optimization_barrier((pair_sum, pick, rim_modes))
        parts = lax.all_to_all(pair_sum, "col", 0, 0, axis_index_groups=SAME_CORE)
        field, *rims = call(
            start_kernel, [held((MODES, TILE), BF16)] + rim_shapes, [VMEM] * 2, [parts, rim_modes], name="start"
        )
        arrived = exchange(rims)
        if repeat == 0:
            now, _ = lax.optimization_barrier((order, field))
            columns = jnp.where(now[0] >= 0, columns, 0)
            cross, coef, rim_coef, links = call(
                link_kernel, [held((4 * TILE, 4 * TILE), BF16), held((8, NE)), held((8, 4 * TILE)), held((4, TILE, TILE), BF16)],
                [SMEM] + [VMEM] * 6, [now, send, receive, pick, real_shift, imag_shift, coupling[0, 0]], name="link", us=0.7,
            )
            local, rim_rest = call(
                open_kernel, [field_shape, rim_shape], [SMEM] + [VMEM] * 5, [columns, field, modes, tiles, pick, residual],
                scratch=tile_scratch, us=1.6, name="open",
            )
        else:
            residual, local, rim_rest = call(
                reopen_kernel, [field_shape, field_shape, rim_shape], [SMEM] + [VMEM] * 7,
                [columns, field, modes, tiles, pick, rest, terms, place],
                scratch=tile_scratch, us=1.6, name="reopen",
            )
        for sweep in range(2):
            terms, *rims = call(
                sweep_kernel, [terms_shape] + rim_shapes, [SMEM] + [VMEM] * 8,
                [inside, *arrived, links, cross, rim_rest, rim_coef], us=0.9, name="sweep",
            )
            arrived = exchange(rims)
            if repeat == 0 and sweep == 0:
                now, _ = lax.optimization_barrier((order, terms))
                place, place_modes = call(
                    place_kernel, [hot_shape, held((MODES, 4 * TILE), BF16)], [SMEM, VMEM, VMEM], [now, receive, modes], name="place"
                )
            common = [residual, local, terms, coef]
            if sweep == 0:
                local, rim_rest = call(
                    middle_kernel, [field_shape, rim_shape], [SMEM] + [VMEM] * 7, [columns, tiles, pick, place] + common,
                    scratch=tile_scratch, us=1.6, name="middle",
                )
            elif repeat + 1 < OUTER:
                solution, rest, projected = call(
                    finish_kernel, [field_shape, field_shape, held((HALF, TILE))], [SMEM] + [VMEM] * 7,
                    [columns, tiles, place] + common + [modes], scratch=tile_scratch, us=1.6, name="finish",
                )
            else:
                solution, rest = call(
                    finish_last_kernel, [shape((ROWS, NE)), field_shape], [SMEM] + [VMEM] * 7,
                    [columns, tiles, place] + common + [solution], scratch=tile_scratch, us=1.6, name="finish_last",
                )
        if repeat + 1 < OUTER:
            terms, packed = call(
                close_kernel, [terms_shape, spread_shape], [SMEM] + [VMEM] * 7,
                [inside, *arrived, links, place_modes, projected], us=0.9, name="close",
            )
        else:
            (residual,) = call(
                last_kernel, [shape((ROWS, NE))], [SMEM] + [VMEM] * 7, [inside, *arrived, links, place, rest],
                us=0.9, name="last", out_specs=[HBM],
                scratch=[pltpu.VMEM((ROWS, NE), F32), pltpu.SemaphoreType.DMA((4,))],
            )
    whole = (1, 1, 2, ROWS // 2, NE)
    return solution.reshape(whole), residual.reshape(whole)


def solution(mesh):
    in_specs = (
        P("row", "col", None, None, None),
        P("row", "col", None),
        P("row", "col", None),
        P("row", "col", None, None, None, None),
        P("row", "col", None, None),
        P("row", "col", None, None, None),
        P("row", "col", None, None),
        P("row", "col", None, None),
        P("row", "col", None, None),
        P("row", "col"),
    )
    out_specs = (P("row", "col", None, None, None), P("row", "col", None, None, None))
    return jax.shard_map(on_device, mesh=mesh, in_specs=in_specs, out_specs=out_specs, check_vma=False)
```

```python
import jax
import jax.numpy as jnp
from jax import lax
from jax.experimental import pallas as pl
from jax.experimental.pallas import tpu as pltpu
from jax.sharding import PartitionSpec as P

OUTER = 2
N = 16
ROWS = 64
NE = 1024
TILE = 128
MODES = 96
HALF = MODES // 2
F32 = jnp.float32
BF16 = jnp.bfloat16
NT = (((1,), (1,)), ((), ()))
TN = (((0,), (0,)), ((), ()))
NN = (((1,), (0,)), ((), ()))

VMEM = pl.BlockSpec(memory_space=pltpu.VMEM)
SMEM = pl.BlockSpec(memory_space=pltpu.SMEM)
HBM = pl.BlockSpec(memory_space=pltpu.HBM)


def dot(a, b, dims):
    return lax.dot_general(a, b, dims, preferred_element_type=F32)


def split(x):
    high = x.astype(BF16).astype(F32)
    return high, x - high


def stacked(x):
    high, low = split(x)
    return jnp.concatenate([high.astype(BF16), low.astype(BF16)], axis=0)


def fold_rows(x):
    return x[:ROWS] + x[ROWS:]


def unpack_modes(x):
    high, low = split(x)
    left = lax.broadcasted_iota(jnp.int32, x.shape, 1) < ROWS
    first = jnp.where(left, high, pltpu.roll(low, ROWS, 1))
    second = jnp.where(left, pltpu.roll(high, ROWS, 1), low)
    return first.astype(BF16), second.astype(BF16)


def pack_modes(first, second):
    left = lax.broadcasted_iota(jnp.int32, first.shape, 1) < ROWS
    return jnp.where(left, first + pltpu.roll(first, ROWS, 1), second + pltpu.roll(second, ROWS, 1))


def project(residual, modes):
    wide = dot(modes, stacked(residual), NT)
    return pack_modes(wide[:HALF], wide[HALF:])


def coefficients(real_shift, imag_shift):
    modulus = real_shift * real_shift + imag_shift * imag_shift
    return real_shift / modulus, imag_shift / modulus


def relax(field, a, b):
    re, im = field[: ROWS // 2], field[ROWS // 2 :]
    return jnp.concatenate([a * re + b * im, a * im - b * re], axis=0)


def spread(packed, out):
    for k in range(N):
        out[k] = packed


def scattered(terms, place):
    return fold_rows(dot(terms, place, NN))


def put_rims(rim, rims):
    for slot in range(4):
        rims[slot][...] = rim[:, slot * TILE : (slot + 1) * TILE]


def project_kernel(residual, modes, out, residual_here, modes_here, sems):
    first = pltpu.make_async_copy(residual, residual_here, sems.at[0])
    second = pltpu.make_async_copy(modes, modes_here, sems.at[1])
    first.start()
    second.start()
    first.wait()
    second.wait()
    spread(project(residual_here[...], modes_here[...]), out)


def one_hot(order, edges, out):
    edge = lax.broadcasted_iota(jnp.int32, (NE, TILE), 0)
    for slot in range(4):
        chosen = edges[pl.ds(order[slot], 1), :]
        out[:, slot * TILE : (slot + 1) * TILE] = jnp.where(edge == chosen, 1.0, 0.0).astype(BF16)


def rim_kernel(order, send, modes, pick, rim_modes):
    one_hot(order, send, pick)
    rim_modes[...] = dot(modes[...], pick[...], NN).astype(BF16)


def link_kernel(order, send, receive, pick, real_shift, imag_shift, coupling, cross, coef, rim_coef, links):
    for slot in range(4):
        links[slot] = coupling[order[slot]].astype(F32).T.astype(BF16)
    targets = targets_of(order, receive)
    for slot in range(4):
        chosen = send[pl.ds(order[slot], 1), :]
        for other in range(4):
            same = targets[:, other : other + 1] == chosen
            cross[other * TILE : (other + 1) * TILE, slot * TILE : (slot + 1) * TILE] = jnp.where(same, 1.0, 0.0).astype(BF16)
    a, b = coefficients(real_shift[...], imag_shift[...])
    both = jnp.concatenate([a, b, jnp.zeros((6, NE), F32)], axis=0)
    coef[...] = both
    total = None
    rest = both
    for _ in range(3):
        term = rest.astype(BF16)
        part = dot(term, pick[...], NN)
        total = part if total is None else total + part
        rest = rest - term.astype(F32)
    rim_coef[...] = total


def targets_of(order, receive):
    rows = [receive[pl.ds(order[slot], 1), :] for slot in range(4)]
    return jnp.concatenate(rows + rows, axis=0).T


def place_kernel(order, receive, modes, place, place_modes):
    targets = targets_of(order, receive)
    edge = lax.broadcasted_iota(jnp.int32, (TILE, NE), 1)
    for slot in range(4):
        same = edge == targets[:, slot : slot + 1]
        place[slot * TILE : (slot + 1) * TILE, :] = jnp.where(same, 1.0, 0.0).astype(BF16)
    place_modes[...] = dot(modes[...], place[...], NT).astype(BF16)


def gather_column(gathered, column):
    for k in range(N):
        first, second = unpack_modes(gathered[k])
        column[k * MODES : k * MODES + HALF, :] = first
        column[k * MODES + HALF : (k + 1) * MODES, :] = second


def half_product(parity, inverse, column, out):
    for k in range(0, N // 2, 4):
        starts = [pl.multiple_of((2 * z + parity) * MODES, MODES) for z in range(k, k + 4)]
        rows = jnp.concatenate([inverse[pl.ds(start, MODES), :] for start in starts], axis=0)
        wide = dot(rows, column[...], NN)
        for z in range(4):
            base = z * MODES
            out[k + z] = pack_modes(wide[base : base + HALF], wide[base + HALF : base + MODES])


def give_kernel(core, gathered, inverse, give, column):
    gather_column(gathered, column)
    half_product(1 - core[0], inverse, column, give)


def keep_kernel(core, column, inverse, keep):
    half_product(core[0], inverse, column, keep)


def start_kernel(parts, rim_modes, field, *rims):
    total = parts[0]
    for k in range(1, N // 2):
        total = total + parts[k]
    first, second = unpack_modes(total)
    both = jnp.concatenate([first, second], axis=0)
    field[...] = both
    put_rims(fold_rows(dot(both, rim_modes[...], TN)), rims)


def tile_product(columns, terms, tiles, scratch):
    for k in range(NE // TILE):
        scratch[k] = terms[:, k * TILE : (k + 1) * TILE]
    pieces = []
    for t in range(NE // TILE):
        taken = jnp.concatenate([scratch[columns[t, k]] for k in range(4)], axis=1)
        stored = jnp.concatenate([tiles[t, k] for k in range(4)], axis=1)
        pieces.append(fold_rows(dot(taken, stored, NT)))
    return jnp.concatenate(pieces, axis=1)


def open_tail(columns, field, modes, tiles, pick, residual, local, rim_rest, scratch):
    update = fold_rows(dot(field[...], modes[...], TN))
    image = tile_product(columns, stacked(update), tiles, scratch)
    local[...] = image
    rim_rest[...] = fold_rows(dot(stacked(residual - image), pick[...], NN))


def open_kernel(columns, field, modes, tiles, pick, residual, local, rim_rest, scratch):
    open_tail(columns, field, modes, tiles, pick, residual[...], local, rim_rest, scratch)


def reopen_kernel(columns, field, modes, tiles, pick, rest, terms, place, residual, local, rim_rest, scratch):
    value = rest[...] - scattered(terms[...], place[...])
    residual[...] = value
    open_tail(columns, field, modes, tiles, pick, value, local, rim_rest, scratch)


def middle_kernel(columns, tiles, pick, place, residual, local, terms, coef, after, rim_rest, scratch):
    whole = residual[...] - (local[...] + scattered(terms[...], place[...]))
    update = relax(whole, coef[0:1, :], coef[1:2, :])
    image = tile_product(columns, stacked(update), tiles, scratch)
    after[...] = image
    rim_rest[...] = fold_rows(dot(stacked(residual[...] - image), pick[...], NN))


def finish(columns, tiles, place, residual, local, terms, coef, scratch):
    applied = local[...] + scattered(terms[...], place[...])
    update = relax(residual[...] - applied, coef[0:1, :], coef[1:2, :])
    return update, applied - tile_product(columns, stacked(update), tiles, scratch)


def finish_kernel(columns, tiles, place, residual, local, terms, coef, modes, solution, rest, projected, scratch):
    update, value = finish(columns, tiles, place, residual, local, terms, coef, scratch)
    solution[...] = update
    rest[...] = value
    projected[...] = project(value, modes[...])


def finish_last_kernel(columns, tiles, place, residual, local, terms, coef, before, solution, rest, scratch):
    update, value = finish(columns, tiles, place, residual, local, terms, coef, scratch)
    solution[...] = before[...] + update
    rest[...] = value


def coupled(inside, rims, links):
    pieces = []
    for slot in range(4):
        offered = jnp.where(inside[slot] > 0, rims[slot][...], 0.0)
        pieces.append(fold_rows(dot(stacked(offered), links[slot], NN)))
    return stacked(jnp.concatenate(pieces, axis=1))


def sweep_kernel(inside, l0, l1, l2, l3, links, cross, rim_rest, rim_coef, terms, *rims):
    value = coupled(inside, (l0, l1, l2, l3), links)
    terms[...] = value
    rest = rim_rest[...] - fold_rows(dot(value, cross[...], NN))
    put_rims(relax(rest, rim_coef[0:1, :], rim_coef[1:2, :]), rims)


def close_kernel(inside, l0, l1, l2, l3, links, place_modes, projected, terms, out):
    value = coupled(inside, (l0, l1, l2, l3), links)
    terms[...] = value
    wide = dot(place_modes[...], value, NT)
    spread(projected[...] - pack_modes(wide[:HALF], wide[HALF:]), out)


def last_kernel(inside, l0, l1, l2, l3, links, place, rest, residual, value, sems):
    terms = coupled(inside, (l0, l1, l2, l3), links)
    copies = []
    for k in range(4):
        lanes = pl.ds(k * 256, 256)
        value[:, lanes] = rest[:, lanes] - scattered(terms, place[:, k * 256 : (k + 1) * 256])
        copies.append(pltpu.make_async_copy(value.at[:, lanes], residual.at[:, lanes], sems.at[k]))
        copies[-1].start()
    for copy in copies:
        copy.wait()


def shape(dims, dtype=F32):
    return jax.ShapeDtypeStruct(dims, dtype)


def held(dims, dtype=F32):
    return pltpu.VMEM(dims, dtype)


def in_hbm(x):
    return pltpu.with_memory_space_constraint(x, pltpu.HBM)


def call(kernel, out_shape, in_specs, args, scratch=(), us=1.0, name=None, limit=16, out_specs=None):
    moved = 2**20
    flops = int(us * 1.1e9)
    return pl.pallas_call(
        kernel,
        out_shape=list(out_shape),
        in_specs=in_specs,
        out_specs=out_specs or [VMEM] * len(out_shape),
        scratch_shapes=list(scratch),
        compiler_params=pltpu.CompilerParams(vmem_limit_bytes=limit * 2**20),
        cost_estimate=pl.CostEstimate(flops=flops, bytes_accessed=moved, transcendentals=0),
        name=name,
    )(*args)


EVEN = [(k, k ^ 1) for k in range(N)]


def odd(k):
    return k - 1 if k % 2 == 0 else k + 1


def permutation(partner):
    return [(N * i + j, N * partner(i, j)[0] + partner(i, j)[1]) for i in range(N) for j in range(N)]


ROW_ODD = permutation(lambda i, j: (i, j ^ 1) if i in (0, N - 1) else (odd(i), j))
COL_ODD = permutation(lambda i, j: (i ^ 1, j) if j in (0, N - 1) else (i, odd(j)))
SAME_CORE = [list(range(core, N, 2)) for core in range(2)]


def on_device(
    excitation,
    shift_real,
    shift_imag,
    local_tiles,
    tile_columns,
    coupling,
    send_edges,
    receive_edges,
    local_modes,
    coarse_inverse,
):
    source = excitation.reshape(ROWS, NE)
    real_shift = shift_real.reshape(1, NE)
    imag_shift = shift_imag.reshape(1, NE)
    tiles = local_tiles[0, 0]
    columns = tile_columns[0, 0]
    send = send_edges[0, 0]
    receive = receive_edges[0, 0]
    modes = local_modes[0, 0]

    row, col = lax.axis_index("row"), lax.axis_index("col")
    row_odd, col_odd = row % 2, col % 2
    order = jnp.stack([row_odd, 2 + col_odd, 1 - row_odd, 3 - col_odd]).astype(jnp.int32)
    one = jnp.ones((), jnp.int32)
    row_in = jnp.where((row > 0) & (row < N - 1), 1, 0).astype(jnp.int32)
    col_in = jnp.where((col > 0) & (col < N - 1), 1, 0).astype(jnp.int32)
    inside = jnp.stack([row_in, col_in, one, one])
    core = col_odd.astype(jnp.int32).reshape(1)

    rim_shapes = [shape((ROWS, TILE))] * 4
    field_shape = held((ROWS, NE))
    rim_shape = held((ROWS, 4 * TILE))
    terms_shape = held((2 * ROWS, 4 * TILE), BF16)
    hot_shape = held((NE, 4 * TILE), BF16)
    spread_shape = shape((N, HALF, TILE))
    half_shape = shape((N // 2, HALF, TILE))

    def exchange(rims):
        return [
            lax.ppermute(rims[0], ("row", "col"), ROW_ODD),
            lax.ppermute(rims[1], ("row", "col"), COL_ODD),
            lax.ppermute(rims[2], "row", EVEN),
            lax.ppermute(rims[3], "col", EVEN),
        ]

    tile_scratch = [pltpu.VMEM((NE // TILE, 2 * ROWS, TILE), BF16)]

    packed, residual, modes = call(
        project_kernel, [spread_shape, field_shape, held((MODES, NE), BF16)], [HBM] * 2, [in_hbm(source), in_hbm(modes)],
        scratch=[pltpu.SemaphoreType.DMA((2,))], name="project", us=8.0,
    )
    packed, order, inside, core = lax.optimization_barrier((packed, order, inside, core))

    for repeat in range(OUTER):
        gathered = lax.all_to_all(packed, "row", 0, 0)
        give, column = call(
            give_kernel, [half_shape, held((N * MODES, TILE), BF16)], [SMEM, VMEM, VMEM], [core, gathered, coarse_inverse],
            us=0.9, name="give",
        )
        (keep,) = call(
            keep_kernel, [half_shape], [SMEM, VMEM, VMEM], [core, column, coarse_inverse], us=0.9, name="keep",
        )
        pair_sum = keep + lax.ppermute(give, "col", EVEN)
        if repeat == 0:
            now, _ = lax.optimization_barrier((order, give))
            pick, rim_modes = call(
                rim_kernel, [hot_shape, held((MODES, 4 * TILE), BF16)], [SMEM, VMEM, VMEM], [now, send, modes], name="rim"
            )
            pair_sum, pick, rim_modes = lax.optimization_barrier((pair_sum, pick, rim_modes))
        parts = lax.all_to_all(pair_sum, "col", 0, 0, axis_index_groups=SAME_CORE)
        field, *rims = call(
            start_kernel, [held((MODES, TILE), BF16)] + rim_shapes, [VMEM] * 2, [parts, rim_modes], name="start"
        )
        arrived = exchange(rims)
        if repeat == 0:
            now, _ = lax.optimization_barrier((order, field))
            columns = jnp.where(now[0] >= 0, columns, 0)
            cross, coef, rim_coef, links = call(
                link_kernel, [held((4 * TILE, 4 * TILE), BF16), held((8, NE)), held((8, 4 * TILE)), held((4, TILE, TILE), BF16)],
                [SMEM] + [VMEM] * 6, [now, send, receive, pick, real_shift, imag_shift, coupling[0, 0]], name="link", us=0.7,
            )
            local, rim_rest = call(
                open_kernel, [field_shape, rim_shape], [SMEM] + [VMEM] * 5, [columns, field, modes, tiles, pick, residual],
                scratch=tile_scratch, us=1.6, name="open",
            )
        else:
            residual, local, rim_rest = call(
                reopen_kernel, [field_shape, field_shape, rim_shape], [SMEM] + [VMEM] * 7,
                [columns, field, modes, tiles, pick, rest, terms, place],
                scratch=tile_scratch, us=1.6, name="reopen",
            )
        for sweep in range(2):
            terms, *rims = call(
                sweep_kernel, [terms_shape] + rim_shapes, [SMEM] + [VMEM] * 8,
                [inside, *arrived, links, cross, rim_rest, rim_coef], us=0.9, name="sweep",
            )
            arrived = exchange(rims)
            if repeat == 0 and sweep == 0:
                now, _ = lax.optimization_barrier((order, terms))
                place, place_modes = call(
                    place_kernel, [held((4 * TILE, NE), BF16), held((MODES, 4 * TILE), BF16)], [SMEM, VMEM, VMEM], [now, receive, modes], name="place"
                )
            common = [residual, local, terms, coef]
            if sweep == 0:
                local, rim_rest = call(
                    middle_kernel, [field_shape, rim_shape], [SMEM] + [VMEM] * 7, [columns, tiles, pick, place] + common,
                    scratch=tile_scratch, us=1.6, name="middle",
                )
            elif repeat + 1 < OUTER:
                solution, rest, projected = call(
                    finish_kernel, [field_shape, field_shape, held((HALF, TILE))], [SMEM] + [VMEM] * 7,
                    [columns, tiles, place] + common + [modes], scratch=tile_scratch, us=1.6, name="finish",
                )
            else:
                solution, rest = call(
                    finish_last_kernel, [shape((ROWS, NE)), field_shape], [SMEM] + [VMEM] * 7,
                    [columns, tiles, place] + common + [solution], scratch=tile_scratch, us=1.6, name="finish_last",
                )
        if repeat + 1 < OUTER:
            terms, packed = call(
                close_kernel, [terms_shape, spread_shape], [SMEM] + [VMEM] * 7,
                [inside, *arrived, links, place_modes, projected], us=0.9, name="close",
            )
        else:
            (residual,) = call(
                last_kernel, [shape((ROWS, NE))], [SMEM] + [VMEM] * 7, [inside, *arrived, links, place, rest],
                us=0.9, name="last", out_specs=[HBM],
                scratch=[pltpu.VMEM((ROWS, NE), F32), pltpu.SemaphoreType.DMA((4,))],
            )
    whole = (1, 1, 2, ROWS // 2, NE)
    return solution.reshape(whole), residual.reshape(whole)


def solution(mesh):
    in_specs = (
        P("row", "col", None, None, None),
        P("row", "col", None),
        P("row", "col", None),
        P("row", "col", None, None, None, None),
        P("row", "col", None, None),
        P("row", "col", None, None, None),
        P("row", "col", None, None),
        P("row", "col", None, None),
        P("row", "col", None, None),
        P("row", "col"),
    )
    out_specs = (P("row", "col", None, None, None), P("row", "col", None, None, None))
    return jax.shard_map(on_device, mesh=mesh, in_specs=in_specs, out_specs=out_specs, check_vma=False)
```

```python
import jax
import jax.numpy as jnp
from jax import lax
from jax.experimental import pallas as pl
from jax.experimental.pallas import tpu as pltpu
from jax.sharding import PartitionSpec as P

OUTER = 2
N = 16
ROWS = 64
NE = 1024
TILE = 128
MODES = 96
HALF = MODES // 2
F32 = jnp.float32
BF16 = jnp.bfloat16
NT = (((1,), (1,)), ((), ()))
TN = (((0,), (0,)), ((), ()))
NN = (((1,), (0,)), ((), ()))

VMEM = pl.BlockSpec(memory_space=pltpu.VMEM)
SMEM = pl.BlockSpec(memory_space=pltpu.SMEM)
HBM = pl.BlockSpec(memory_space=pltpu.HBM)


def dot(a, b, dims):
    return lax.dot_general(a, b, dims, preferred_element_type=F32)


def split(x):
    high = x.astype(BF16).astype(F32)
    return high, x - high


def stacked(x):
    high, low = split(x)
    return jnp.concatenate([high.astype(BF16), low.astype(BF16)], axis=0)


def fold_rows(x):
    return x[:ROWS] + x[ROWS:]


def unpack_modes(x):
    high, low = split(x)
    left = lax.broadcasted_iota(jnp.int32, x.shape, 1) < ROWS
    first = jnp.where(left, high, pltpu.roll(low, ROWS, 1))
    second = jnp.where(left, pltpu.roll(high, ROWS, 1), low)
    return first.astype(BF16), second.astype(BF16)


def pack_modes(first, second):
    left = lax.broadcasted_iota(jnp.int32, first.shape, 1) < ROWS
    return jnp.where(left, first + pltpu.roll(first, ROWS, 1), second + pltpu.roll(second, ROWS, 1))


def project(residual, modes):
    wide = dot(modes, stacked(residual), NT)
    return pack_modes(wide[:HALF], wide[HALF:])


def coefficients(real_shift, imag_shift):
    modulus = real_shift * real_shift + imag_shift * imag_shift
    return real_shift / modulus, imag_shift / modulus


def relax(field, a, b):
    re, im = field[: ROWS // 2], field[ROWS // 2 :]
    return jnp.concatenate([a * re + b * im, a * im - b * re], axis=0)


def spread(packed, out):
    for k in range(N):
        out[k] = packed


def scattered(terms, place):
    return fold_rows(dot(terms, place, NN))


def put_rims(rim, rims):
    for slot in range(4):
        rims[slot][...] = rim[:, slot * TILE : (slot + 1) * TILE]


def project_kernel(residual, modes, out, residual_here, modes_here, sems):
    first = pltpu.make_async_copy(residual, residual_here, sems.at[0])
    second = pltpu.make_async_copy(modes, modes_here, sems.at[1])
    first.start()
    second.start()
    first.wait()
    second.wait()
    spread(project(residual_here[...], modes_here[...]), out)


def one_hot(order, edges, out):
    edge = lax.broadcasted_iota(jnp.int32, (NE, TILE), 0)
    for slot in range(4):
        chosen = edges[pl.ds(order[slot], 1), :]
        out[:, slot * TILE : (slot + 1) * TILE] = jnp.where(edge == chosen, 1.0, 0.0).astype(BF16)


def rim_kernel(order, send, modes, pick, rim_modes):
    one_hot(order, send, pick)
    rim_modes[...] = dot(modes[...], pick[...], NN).astype(BF16)


def link_kernel(order, send, receive, pick, real_shift, imag_shift, coupling, cross, coef, rim_coef, links):
    for slot in range(4):
        links[slot] = coupling[order[slot]].astype(F32).T.astype(BF16)
    targets = targets_of(order, receive)
    for slot in range(4):
        chosen = send[pl.ds(order[slot], 1), :]
        for other in range(4):
            same = targets[:, other : other + 1] == chosen
            cross[other * TILE : (other + 1) * TILE, slot * TILE : (slot + 1) * TILE] = jnp.where(same, 1.0, 0.0).astype(BF16)
    a, b = coefficients(real_shift[...], imag_shift[...])
    both = jnp.concatenate([a, b, jnp.zeros((6, NE), F32)], axis=0)
    coef[...] = both
    total = None
    rest = both
    for _ in range(3):
        term = rest.astype(BF16)
        part = dot(term, pick[...], NN)
        total = part if total is None else total + part
        rest = rest - term.astype(F32)
    rim_coef[...] = total


def targets_of(order, receive):
    rows = [receive[pl.ds(order[slot], 1), :] for slot in range(4)]
    return jnp.concatenate(rows + rows, axis=0).T


def place_kernel(order, receive, modes, place, place_modes):
    targets = targets_of(order, receive)
    edge = lax.broadcasted_iota(jnp.int32, (TILE, NE), 1)
    for slot in range(4):
        same = edge == targets[:, slot : slot + 1]
        place[slot * TILE : (slot + 1) * TILE, :] = jnp.where(same, 1.0, 0.0).astype(BF16)
    place_modes[...] = dot(modes[...], place[...], NT).astype(BF16)


def gather_column(gathered, column):
    for k in range(N):
        first, second = unpack_modes(gathered[k])
        column[k * MODES : k * MODES + HALF, :] = first
        column[k * MODES + HALF : (k + 1) * MODES, :] = second


def half_product(parity, inverse, column, out):
    for k in range(0, N // 2, 4):
        starts = [pl.multiple_of((2 * z + parity) * MODES, MODES) for z in range(k, k + 4)]
        rows = jnp.concatenate([inverse[pl.ds(start, MODES), :] for start in starts], axis=0)
        wide = dot(rows, column[...], NN)
        for z in range(4):
            base = z * MODES
            out[k + z] = pack_modes(wide[base : base + HALF], wide[base + HALF : base + MODES])


def give_kernel(core, gathered, inverse, give, column):
    gather_column(gathered, column)
    half_product(1 - core[0], inverse, column, give)


def keep_kernel(core, column, inverse, keep):
    half_product(core[0], inverse, column, keep)


def start_kernel(parts, rim_modes, field, *rims):
    total = parts[0]
    for k in range(1, N // 2):
        total = total + parts[k]
    first, second = unpack_modes(total)
    both = jnp.concatenate([first, second], axis=0)
    field[...] = both
    put_rims(fold_rows(dot(both, rim_modes[...], TN)), rims)


def tile_product(columns, terms, tiles, scratch):
    for k in range(NE // TILE):
        scratch[k] = terms[:, k * TILE : (k + 1) * TILE]
    pieces = []
    for t in range(NE // TILE):
        taken = jnp.concatenate([scratch[columns[t, k]] for k in range(4)], axis=1)
        stored = jnp.concatenate([tiles[t, k] for k in range(4)], axis=1)
        pieces.append(fold_rows(dot(taken, stored, NT)))
    return jnp.concatenate(pieces, axis=1)


def open_tail(columns, field, modes, tiles, pick, residual, local, rim_rest, scratch):
    update = fold_rows(dot(field[...], modes[...], TN))
    image = tile_product(columns, stacked(update), tiles, scratch)
    local[...] = image
    rim_rest[...] = fold_rows(dot(stacked(residual - image), pick[...], NN))


def open_kernel(columns, field, modes, tiles, pick, residual, local, rim_rest, scratch):
    open_tail(columns, field, modes, tiles, pick, residual[...], local, rim_rest, scratch)


def reopen_kernel(columns, field, modes, tiles, pick, rest, terms, place, residual, local, rim_rest, scratch):
    value = rest[...] - scattered(terms[...], place[...])
    residual[...] = value
    open_tail(columns, field, modes, tiles, pick, value, local, rim_rest, scratch)


def middle_kernel(columns, tiles, pick, place, residual, local, terms, coef, after, rim_rest, scratch):
    whole = residual[...] - (local[...] + scattered(terms[...], place[...]))
    update = relax(whole, coef[0:1, :], coef[1:2, :])
    image = tile_product(columns, stacked(update), tiles, scratch)
    after[...] = image
    rim_rest[...] = fold_rows(dot(stacked(residual[...] - image), pick[...], NN))


def finish(columns, tiles, place, residual, local, terms, coef, scratch):
    applied = local[...] + scattered(terms[...], place[...])
    update = relax(residual[...] - applied, coef[0:1, :], coef[1:2, :])
    return update, applied - tile_product(columns, stacked(update), tiles, scratch)


def finish_kernel(columns, tiles, place, residual, local, terms, coef, modes, solution, rest, projected, scratch):
    update, value = finish(columns, tiles, place, residual, local, terms, coef, scratch)
    solution[...] = update
    rest[...] = value
    projected[...] = project(value, modes[...])


def finish_last_kernel(columns, tiles, place, residual, local, terms, coef, before, solution, rest, scratch):
    update, value = finish(columns, tiles, place, residual, local, terms, coef, scratch)
    solution[...] = before[...] + update
    rest[...] = value


def coupled(inside, rims, links):
    pieces = []
    for slot in range(4):
        offered = jnp.where(inside[slot] > 0, rims[slot][...], 0.0)
        pieces.append(fold_rows(dot(stacked(offered), links[slot], NN)))
    return stacked(jnp.concatenate(pieces, axis=1))


def sweep_kernel(inside, l0, l1, l2, l3, links, cross, rim_rest, rim_coef, terms, *rims):
    value = coupled(inside, (l0, l1, l2, l3), links)
    terms[...] = value
    rest = rim_rest[...] - fold_rows(dot(value, cross[...], NN))
    put_rims(relax(rest, rim_coef[0:1, :], rim_coef[1:2, :]), rims)


def close_kernel(inside, l0, l1, l2, l3, links, place_modes, projected, terms, out):
    value = coupled(inside, (l0, l1, l2, l3), links)
    terms[...] = value
    wide = dot(place_modes[...], value, NT)
    spread(projected[...] - pack_modes(wide[:HALF], wide[HALF:]), out)


def last_kernel(inside, l0, l1, l2, l3, links, place, rest, residual, value, sems):
    terms = coupled(inside, (l0, l1, l2, l3), links)
    copies = []
    for k in range(4):
        lanes = pl.ds(k * 256, 256)
        value[:, lanes] = rest[:, lanes] - scattered(terms, place[:, k * 256 : (k + 1) * 256])
        copies.append(pltpu.make_async_copy(value.at[:, lanes], residual.at[:, lanes], sems.at[k]))
        copies[-1].start()
    for copy in copies:
        copy.wait()


def shape(dims, dtype=F32):
    return jax.ShapeDtypeStruct(dims, dtype)


def held(dims, dtype=F32):
    return pltpu.VMEM(dims, dtype)


def in_hbm(x):
    return pltpu.with_memory_space_constraint(x, pltpu.HBM)


def call(kernel, out_shape, in_specs, args, scratch=(), us=1.0, name=None, limit=16, out_specs=None):
    moved = 2**20
    flops = int(us * 1.1e9)
    return pl.pallas_call(
        kernel,
        out_shape=list(out_shape),
        in_specs=in_specs,
        out_specs=out_specs or [VMEM] * len(out_shape),
        scratch_shapes=list(scratch),
        compiler_params=pltpu.CompilerParams(vmem_limit_bytes=limit * 2**20),
        cost_estimate=pl.CostEstimate(flops=flops, bytes_accessed=moved, transcendentals=0),
        name=name,
    )(*args)


EVEN = [(k, k ^ 1) for k in range(N)]


def odd(k):
    return k - 1 if k % 2 == 0 else k + 1


def permutation(partner):
    return [(N * i + j, N * partner(i, j)[0] + partner(i, j)[1]) for i in range(N) for j in range(N)]


ROW_ODD = permutation(lambda i, j: (i, j ^ 1) if i in (0, N - 1) else (odd(i), j))
COL_ODD = permutation(lambda i, j: (i ^ 1, j) if j in (0, N - 1) else (i, odd(j)))
SAME_CORE = [list(range(core, N, 2)) for core in range(2)]


def on_device(
    excitation,
    shift_real,
    shift_imag,
    local_tiles,
    tile_columns,
    coupling,
    send_edges,
    receive_edges,
    local_modes,
    coarse_inverse,
):
    source = excitation.reshape(ROWS, NE)
    real_shift = shift_real.reshape(1, NE)
    imag_shift = shift_imag.reshape(1, NE)
    tiles = local_tiles[0, 0]
    columns = tile_columns[0, 0]
    send = send_edges[0, 0]
    receive = receive_edges[0, 0]
    modes = local_modes[0, 0]

    row, col = lax.axis_index("row"), lax.axis_index("col")
    row_odd, col_odd = row % 2, col % 2
    order = jnp.stack([row_odd, 1 - row_odd, 2 + col_odd, 3 - col_odd]).astype(jnp.int32)
    one = jnp.ones((), jnp.int32)
    row_in = jnp.where((row > 0) & (row < N - 1), 1, 0).astype(jnp.int32)
    col_in = jnp.where((col > 0) & (col < N - 1), 1, 0).astype(jnp.int32)
    inside = jnp.stack([row_in, one, col_in, one])
    core = col_odd.astype(jnp.int32).reshape(1)

    rim_shapes = [shape((ROWS, TILE))] * 4
    field_shape = held((ROWS, NE))
    rim_shape = held((ROWS, 4 * TILE))
    terms_shape = held((2 * ROWS, 4 * TILE), BF16)
    hot_shape = held((NE, 4 * TILE), BF16)
    spread_shape = shape((N, HALF, TILE))
    half_shape = shape((N // 2, HALF, TILE))

    def exchange(rims):
        return [
            lax.ppermute(rims[0], ("row", "col"), ROW_ODD),
            lax.ppermute(rims[1], "row", EVEN),
            lax.ppermute(rims[2], ("row", "col"), COL_ODD),
            lax.ppermute(rims[3], "col", EVEN),
        ]

    tile_scratch = [pltpu.VMEM((NE // TILE, 2 * ROWS, TILE), BF16)]

    packed, residual, modes = call(
        project_kernel, [spread_shape, field_shape, held((MODES, NE), BF16)], [HBM] * 2, [in_hbm(source), in_hbm(modes)],
        scratch=[pltpu.SemaphoreType.DMA((2,))], name="project", us=8.0,
    )
    packed, order, inside, core = lax.optimization_barrier((packed, order, inside, core))

    for repeat in range(OUTER):
        gathered = lax.all_to_all(packed, "row", 0, 0)
        give, column = call(
            give_kernel, [half_shape, held((N * MODES, TILE), BF16)], [SMEM, VMEM, VMEM], [core, gathered, coarse_inverse],
            us=0.9, name="give",
        )
        (keep,) = call(
            keep_kernel, [half_shape], [SMEM, VMEM, VMEM], [core, column, coarse_inverse], us=0.9, name="keep",
        )
        pair_sum = keep + lax.ppermute(give, "col", EVEN)
        if repeat == 0:
            now, _ = lax.optimization_barrier((order, give))
            pick, rim_modes = call(
                rim_kernel, [hot_shape, held((MODES, 4 * TILE), BF16)], [SMEM, VMEM, VMEM], [now, send, modes], name="rim"
            )
            pair_sum, pick, rim_modes = lax.optimization_barrier((pair_sum, pick, rim_modes))
        parts = lax.all_to_all(pair_sum, "col", 0, 0, axis_index_groups=SAME_CORE)
        field, *rims = call(
            start_kernel, [held((MODES, TILE), BF16)] + rim_shapes, [VMEM] * 2, [parts, rim_modes], name="start"
        )
        arrived = exchange(rims)
        if repeat == 0:
            now, _ = lax.optimization_barrier((order, field))
            columns = jnp.where(now[0] >= 0, columns, 0)
            cross, coef, rim_coef, links = call(
                link_kernel, [held((4 * TILE, 4 * TILE), BF16), held((8, NE)), held((8, 4 * TILE)), held((4, TILE, TILE), BF16)],
                [SMEM] + [VMEM] * 6, [now, send, receive, pick, real_shift, imag_shift, coupling[0, 0]], name="link", us=0.7,
            )
            local, rim_rest = call(
                open_kernel, [field_shape, rim_shape], [SMEM] + [VMEM] * 5, [columns, field, modes, tiles, pick, residual],
                scratch=tile_scratch, us=1.6, name="open",
            )
        else:
            residual, local, rim_rest = call(
                reopen_kernel, [field_shape, field_shape, rim_shape], [SMEM] + [VMEM] * 7,
                [columns, field, modes, tiles, pick, rest, terms, place],
                scratch=tile_scratch, us=1.6, name="reopen",
            )
        for sweep in range(2):
            terms, *rims = call(
                sweep_kernel, [terms_shape] + rim_shapes, [SMEM] + [VMEM] * 8,
                [inside, *arrived, links, cross, rim_rest, rim_coef], us=0.9, name="sweep",
            )
            arrived = exchange(rims)
            if repeat == 0 and sweep == 0:
                now, _ = lax.optimization_barrier((order, terms))
                place, place_modes = call(
                    place_kernel, [held((4 * TILE, NE), BF16), held((MODES, 4 * TILE), BF16)], [SMEM, VMEM, VMEM], [now, receive, modes], name="place"
                )
            common = [residual, local, terms, coef]
            if sweep == 0:
                local, rim_rest = call(
                    middle_kernel, [field_shape, rim_shape], [SMEM] + [VMEM] * 7, [columns, tiles, pick, place] + common,
                    scratch=tile_scratch, us=1.6, name="middle",
                )
            elif repeat + 1 < OUTER:
                solution, rest, projected = call(
                    finish_kernel, [field_shape, field_shape, held((HALF, TILE))], [SMEM] + [VMEM] * 7,
                    [columns, tiles, place] + common + [modes], scratch=tile_scratch, us=1.6, name="finish",
                )
            else:
                solution, rest = call(
                    finish_last_kernel, [shape((ROWS, NE)), field_shape], [SMEM] + [VMEM] * 7,
                    [columns, tiles, place] + common + [solution], scratch=tile_scratch, us=1.6, name="finish_last",
                )
        if repeat + 1 < OUTER:
            terms, packed = call(
                close_kernel, [terms_shape, spread_shape], [SMEM] + [VMEM] * 7,
                [inside, *arrived, links, place_modes, projected], us=0.9, name="close",
            )
        else:
            (residual,) = call(
                last_kernel, [shape((ROWS, NE))], [SMEM] + [VMEM] * 7, [inside, *arrived, links, place, rest],
                us=0.9, name="last", out_specs=[HBM],
                scratch=[pltpu.VMEM((ROWS, NE), F32), pltpu.SemaphoreType.DMA((4,))],
            )
    whole = (1, 1, 2, ROWS // 2, NE)
    return solution.reshape(whole), residual.reshape(whole)


def solution(mesh):
    in_specs = (
        P("row", "col", None, None, None),
        P("row", "col", None),
        P("row", "col", None),
        P("row", "col", None, None, None, None),
        P("row", "col", None, None),
        P("row", "col", None, None, None),
        P("row", "col", None, None),
        P("row", "col", None, None),
        P("row", "col", None, None),
        P("row", "col"),
    )
    out_specs = (P("row", "col", None, None, None), P("row", "col", None, None, None))
    return jax.shard_map(on_device, mesh=mesh, in_specs=in_specs, out_specs=out_specs, check_vma=False)
```
